256 devices in a mesh: row: 32 (over y, z_hi, core), blk: 8 (over z_lo, x).
Axes of the slice: x: 4, y: 4, z: 8 (z_hi: 4, z_lo: 2; z = z_hi * 2 + z_lo), core: 2. Of those that a mesh axis runs over, the one named last changes fastest.
Arguments:
- points: float32 [16, 65536], P(None, ('row', 'blk')), may hold values from 0 to 1
- lengthscales: float32 [16], replicated, may hold values from 0.4 to 0.6
- point_order: int32 [65536], replicated, may hold values from 0 to 65535, each once
- block_slot: int32 [64], replicated, may hold values from 0 to 63, each once
- block_inverses: bfloat16 [64, 1024, 1024], P('row', 'blk'), may hold values from -0.1875 to 0.1875
- residual: float32 [64, 64, 1024], P(None, 'row'), may hold values from -6 to 6
Outputs:
- increments: bfloat16 [64, 64, 1024], P(None, 'row', 'blk')
- new_residual: float32 [64, 65536], P(None, ('row', 'blk'))
The draws below stay inside these ranges and needn't reach their ends.
All inputs are finite; a program needn't handle non-finite values.
Results may differ from the reference program's by a relative error of at most 0.0049.
Values may be sent and summed in bfloat16 or wider, within the bound.
No kernel may reach another device: no remote copies, remote signals or barrier semaphores. Data moves between devices by JAX's collectives and lax.ppermute only.
A program may use at most 192 MiB of HBM per device.

```python
import math
import jax
import jax.numpy as jnp
from jax import lax

BS = 1024
COLS = 64
DIM = 16
NB = 64
N = 65536


def block_scale(rng, dims, shards, low, high):
    gain, own = 1.0, jax.random.fold_in(rng, 6)
    for dim, shards_of in shards:
        heights = jnp.exp(jax.random.uniform(jax.random.fold_in(own, dim), (shards_of,), jnp.float32, low / len(shards), high / len(shards)))
        gain = gain * jnp.repeat(heights, dims[dim] // shards_of).reshape([-1 if axis == dim else 1 for axis in range(len(dims))])
    return gain


def bell_draw(own_key, shape, width, limit, split=(), held_as=jnp.bfloat16):
    entries = jax.random.normal(own_key, shape, jnp.float32) * width
    if len(split) > 0:
        entries = block_scale(own_key, shape, split, -0.22, 0.18) * entries
    return jnp.clip(entries, min=-limit, max=limit).astype(held_as)


def setup_inputs(seed: int = 0) -> dict:
    arg_keys = jax.random.split(jax.random.key(seed), 7)
    return {
        "points": jnp.clip(1.0 * jax.random.uniform(arg_keys[0], (DIM, N), jnp.float32) ** block_scale(arg_keys[0], (DIM, N), ((1, 256),), -0.2, 0.2), 0.0, 1.0),
        "lengthscales": jnp.clip(jnp.exp(jax.random.uniform(arg_keys[1], (DIM,), jnp.float32, math.log(0.4), math.log(0.6))), 0.4, 0.6),
        "point_order": jax.random.permutation(arg_keys[2], N).astype(jnp.int32),
        "block_slot": jax.random.permutation(arg_keys[3], NB).astype(jnp.int32),
        "block_inverses": bell_draw(arg_keys[4], (NB, BS, BS), BS ** -0.5, 0.1875, ((0, 32), (1, 8))),
        "residual": bell_draw(arg_keys[5], (COLS, NB, BS), 1.0, 6.0, ((1, 32),), jnp.float32),
    }


damping = 0.5
amplitude = 0.3
noise_var = 0.25


def reference(points, lengthscales, point_order, block_slot, block_inverses, residual):
    scaled = points / lengthscales[:, None]
    offsets = jnp.arange(BS, dtype=jnp.int32)
    slot_points = point_order[(block_slot[:, None] * BS + offsets[None, :]).astype(jnp.int32)]
    coords = jnp.take(scaled, slot_points.reshape(-1), axis=1)
    sqnorm = jnp.sum(coords * coords, axis=0)
    res_low = residual.astype(jnp.bfloat16)
    solved = jnp.einsum("sij,csj->csi", block_inverses.astype(jnp.float32), res_low.astype(jnp.float32), precision=lax.Precision.HIGHEST)
    increments = (damping * solved).astype(jnp.bfloat16)
    flat_inc = increments.reshape(COLS, N)

    def row_block(index):
        target = lax.dynamic_slice_in_dim(coords, (index * BS).astype(jnp.int32), BS, 1)
        target_sq = lax.dynamic_slice_in_dim(sqnorm, (index * BS).astype(jnp.int32), BS, 0)
        cross = jnp.dot(coords.T, target, precision=lax.Precision.HIGHEST, preferred_element_type=jnp.float32)
        dist = sqnorm[:, None] + target_sq[None, :] - 2.0 * cross
        kernel = (amplitude * jnp.exp(-0.5 * dist)).astype(jnp.bfloat16)
        return jnp.dot(flat_inc, kernel, preferred_element_type=jnp.float32)

    changes = lax.map(row_block, jnp.arange(NB, dtype=jnp.int32))
    change = jnp.transpose(changes, (1, 0, 2)).reshape(COLS, N) + noise_var * flat_inc.astype(jnp.float32)
    new_residual = residual.reshape(COLS, N) - change
    return increments, new_residual
```

```python
import math

import jax
import jax.numpy as jnp
import numpy as np
from jax import lax
from jax.experimental import pallas as pl
from jax.experimental.pallas import tpu as pltpu
from jax.sharding import Mesh
from jax.sharding import PartitionSpec as P

damping = 0.5
amplitude = 0.3
noise_var = 0.25

AXES = ("y", "zh", "core", "zl", "x")
SIZES = (4, 4, 2, 2, 4)
DIM = 16
COLS = 64
PART = 256
BS = 1024
NBLK = 64
LANES = 128
ZS = 8
XY = 16
LOG2E = math.log2(math.e)
LOG2AMP = math.log2(amplitude)

VM = pl.BlockSpec(memory_space=pltpu.VMEM)
SM = pl.BlockSpec(memory_space=pltpu.SMEM)


def place(f):
    return (
        lax.shift_right_logical(f, 6),
        lax.shift_right_logical(f, 4) & 3,
        lax.shift_right_logical(f, 3) & 1,
        lax.shift_right_logical(f, 2) & 1,
        f & 3,
    )


def solve_kernel(inv_ref, res_ref, inc_ref, flat_ref):
    for s in range(2):
        low = res_ref[:, s, :].astype(jnp.bfloat16)
        solved = lax.dot_general(
            low, inv_ref[s], (((1,), (1,)), ((), ())), preferred_element_type=jnp.float32
        )
        inc = (damping * solved).astype(jnp.bfloat16)
        inc_ref[:, s, :] = inc
        flat_ref[:, s * LANES : (s + 1) * LANES] = inc


def pick_kernel(flat_ref, slot_ref, order_ref, mine_ref, other_ref, out_ref):
    y, zh, core, zl, x = place(flat_ref[0])

    def one_peer(peer, carry):
        peer_zh, peer_zl = lax.shift_right_logical(peer, 1), peer & 1
        slot = 2 * ((y * 4 + peer_zh) * 2 + core)
        rows = [
            slot_ref[slot] * 8 + peer_zl * 4 + x,
            slot_ref[slot + 1] * 8 + peer_zl * 4 + x,
            slot_ref[slot + peer_zl] * 8 + 2 * x,
            slot_ref[slot + peer_zl] * 8 + 2 * x + 1,
        ]
        tiles, lanes = [], []
        for row in rows:
            p = jnp.broadcast_to(order_ref[pl.ds(row, 1), :], (8, LANES))
            g = lax.shift_right_logical(p, 8)
            gy, gzh, gcore, gzl, gx = place(g)
            half = lax.shift_right_logical(p, 7) & 1
            tile = (((gcore ^ core) * 4 + gx) * 4 + gy) * 2 + half
            tiles.append(jnp.where((gzh == zh) & (gzl == zl), tile, -1))
            lanes.append(p & (LANES - 1))
        found = [[jnp.zeros((8, LANES), jnp.float32) for _ in range(2)] for _ in rows]
        for index in range(2 * XY * 2):
            table = mine_ref if index < 2 * XY else other_ref
            dev, half = (index // 2) % XY, index % 2
            for d in range(2):
                values = table[dev, d * 8 : d * 8 + 8, half * LANES : (half + 1) * LANES]
                for k in range(4):
                    taken = jnp.take_along_axis(values, lanes[k], axis=1)
                    found[k][d] = jnp.where(tiles[k] == index, taken, found[k][d])
        for k in range(4):
            for d in range(2):
                out_ref[peer, k // 2, d * 8 : d * 8 + 8, (k % 2) * LANES : (k % 2 + 1) * LANES] = found[k][d]
        return carry

    lax.fori_loop(0, ZS, one_peer, 0)


def pack_kernel(parts_ref, inc_ref, rows_ref, cols_ref):
    own = jnp.sum(parts_ref[:, 0], axis=0)
    high = own.astype(jnp.bfloat16)
    rows_ref[0:COLS, :] = inc_ref[...]
    rows_ref[COLS : COLS + DIM, :] = high
    rows_ref[COLS + DIM :, :] = (own - high.astype(jnp.float32)).astype(jnp.bfloat16)
    target = jnp.sum(parts_ref[:, 1], axis=0)
    high = target.astype(jnp.bfloat16)
    cols_ref[0:DIM, :] = high
    cols_ref[DIM:, :] = (target - high.astype(jnp.float32)).astype(jnp.bfloat16)


def three_terms(value):
    first = value.astype(jnp.bfloat16).astype(jnp.float32)
    second = (value - first).astype(jnp.bfloat16).astype(jnp.float32)
    return first, second, value - first - second


def features(high, low, left, extra):
    full = high.astype(jnp.float32) + low.astype(jnp.float32)
    norm = extra - 0.5 * jnp.sum(full * full, axis=0, keepdims=True)
    first, second, third = three_terms(norm)
    row = lax.broadcasted_iota(jnp.int32, high.shape, 0)
    base = 0 if left else 3
    tail = jnp.where((row >= 3 - base) & (row < 6 - base), 1.0, 0.0)
    tail = jnp.where(row == base, first, tail)
    tail = jnp.where(row == base + 1, second, tail)
    tail = jnp.where(row == base + 2, third, tail)
    tail = tail.astype(jnp.bfloat16)
    pieces = [high, low, high, low, tail] if left else [high, high, low, low, tail]
    return jnp.concatenate(pieces, axis=0)


FEATURES = 5 * DIM
TILE = 512


def main_kernel(flat_ref, mine_ref, other_ref, cols_ref, out_ref, right_ref):
    y, zh, core, zl, x = place(flat_ref[0])
    for peer in range(ZS):
        right_ref[:, peer * PART : (peer + 1) * PART] = features(
            cols_ref[peer, :DIM], cols_ref[peer, DIM:], False, LOG2AMP
        )
    out_ref[...] = jnp.zeros_like(out_ref)

    def one_device(dev, source):
        block = source[dev]
        values = block[:COLS]
        left = features(block[COLS : COLS + DIM], block[COLS + DIM :], True, 0.0)
        for tile in range(ZS * PART // TILE):
            exponent = lax.dot_general(
                left,
                right_ref[:, tile * TILE : (tile + 1) * TILE],
                (((0,), (0,)), ((), ())),
                preferred_element_type=jnp.float32,
            )
            entries = jnp.exp2(exponent).astype(jnp.bfloat16)
            part = jnp.dot(values, entries, preferred_element_type=jnp.float32)
            for k in range(TILE // PART):
                out_ref[tile * (TILE // PART) + k] += part[:, k * PART : (k + 1) * PART]

    def step(dev, carry):
        one_device(dev, mine_ref)
        one_device(dev, other_ref)
        return carry

    lax.fori_loop(0, XY, step, 0)

    @pl.when(lax.shift_right_logical(x, 1) == zl)
    def _():
        for j in range(2):
            dev = (2 * (x & 1) + j) * 4 + y
            for s in range(2):
                noise = noise_var * mine_ref[dev, 0:COLS, s * LANES : (s + 1) * LANES].astype(jnp.float32)
                out_ref[zh * 2 + s, :, j * LANES : (j + 1) * LANES] += noise


def spread(value, axes, count):
    copies = jnp.broadcast_to(value, (count, *value.shape))
    return lax.all_to_all(copies, axes, split_axis=0, concat_axis=0, tiled=True)


def swap_core(value):
    return lax.ppermute(value, "core", [(0, 1), (1, 0)])


def call(kernel, shapes, in_specs, scratch=()):
    return pl.pallas_call(
        kernel,
        out_shape=shapes,
        in_specs=in_specs,
        out_specs=jax.tree.map(lambda _: VM, shapes),
        scratch_shapes=scratch,
    )


def per_device(points, lengthscales, point_order, block_slot, block_inverses, residual):
    f32, bf16, shape = jnp.float32, jnp.bfloat16, jax.ShapeDtypeStruct
    flat = lax.axis_index(AXES).astype(jnp.int32)
    _, _, _, zl, x = place(flat)
    flat = flat[None]
    own_points = (points - 0.5) * (math.sqrt(LOG2E) / lengthscales)[:, None]
    mine = spread(own_points, ("x", "y"), XY)
    other = swap_core(mine)
    increments, flat_inc = call(
        solve_kernel, (shape((COLS, 2, LANES), bf16), shape((COLS, PART), bf16)), [VM, VM]
    )(block_inverses, residual)
    picked = call(pick_kernel, shape((ZS, 2, DIM, PART), f32), [SM, SM, VM, VM, VM])(
        flat, block_slot, point_order.reshape(-1, LANES), mine, other
    )
    parts = lax.all_to_all(picked, ("zh", "zl"), split_axis=0, concat_axis=0, tiled=True)
    row_pack, col_pack = call(
        pack_kernel, (shape((COLS + 2 * DIM, PART), bf16), shape((2 * DIM, PART), bf16)), [VM, VM]
    )(parts, flat_inc)
    rows_mine = spread(row_pack, ("x", "y"), XY)
    rows_other = swap_core(rows_mine)
    cols = spread(col_pack, ("zh", "zl"), ZS)
    partial = call(
        main_kernel,
        shape((ZS, COLS, PART), f32),
        [SM, VM, VM, VM],
        [pltpu.VMEM((FEATURES, ZS * PART), bf16)],
    )(flat, rows_mine, rows_other, cols)
    change = lax.all_to_all(partial, ("zh", "zl"), split_axis=0, concat_axis=0, tiled=True).sum(axis=0)
    old = lax.dynamic_slice(residual, (0, zl, x * PART), (COLS, 1, PART)).reshape(COLS, PART)
    return increments, old - change


def solution(mesh):
    fine = Mesh(np.asarray(mesh.devices).reshape(SIZES), AXES)
    row, blk = ("y", "zh", "core"), ("zl", "x")
    return jax.shard_map(
        per_device,
        mesh=fine,
        in_specs=(P(None, AXES), P(), P(), P(), P(row, blk, None), P(None, row, None)),
        out_specs=(P(None, row, blk), P(None, AXES)),
        check_vma=False,
    )
```

```python
import math

import jax
import jax.numpy as jnp
import numpy as np
from jax import lax
from jax.experimental import pallas as pl
from jax.experimental.pallas import tpu as pltpu
from jax.sharding import Mesh
from jax.sharding import PartitionSpec as P

damping = 0.5
amplitude = 0.3
noise_var = 0.25

AXES = ("y", "zh", "core", "zl", "x")
SIZES = (4, 4, 2, 2, 4)
DIM = 16
COLS = 64
PART = 256
BS = 1024
NBLK = 64
LANES = 128
ZS = 8
XY = 16
KERNEL_VMEM = 16 << 20
LOG2E = math.log2(math.e)
LOG2AMP = math.log2(amplitude)

VM = pl.BlockSpec(memory_space=pltpu.VMEM)
SM = pl.BlockSpec(memory_space=pltpu.SMEM)


def place(f):
    return (
        lax.shift_right_logical(f, 6),
        lax.shift_right_logical(f, 4) & 3,
        lax.shift_right_logical(f, 3) & 1,
        lax.shift_right_logical(f, 2) & 1,
        f & 3,
    )


def solve_kernel(inv_ref, res_ref, inc_ref, flat_ref):
    for s in range(2):
        low = res_ref[:, s, :].astype(jnp.bfloat16)
        solved = lax.dot_general(
            low, inv_ref[s], (((1,), (1,)), ((), ())), preferred_element_type=jnp.float32
        )
        inc = (damping * solved).astype(jnp.bfloat16)
        inc_ref[:, s, :] = inc
        flat_ref[:, s * LANES : (s + 1) * LANES] = inc


def start_kernel(scale_ref, points_ref, out_ref):
    scale = jnp.concatenate([jnp.full((1, PART), scale_ref[d], jnp.float32) for d in range(DIM)], axis=0)
    own = (points_ref[...] - 0.5) * (math.sqrt(LOG2E) / scale)
    high = own.astype(jnp.bfloat16)
    low = (own - high.astype(jnp.float32)).astype(jnp.bfloat16)
    for dev in range(XY):
        out_ref[dev, :DIM, :] = high
        out_ref[dev, DIM:, :] = low


def pick_kernel(flat_ref, slot_ref, order_ref, mine_ref, other_ref, _, out_ref):
    y, zh, core, zl, x = place(flat_ref[0])
    member = lax.broadcasted_iota(jnp.int32, (PART, 2 * PART), 0)

    def one_peer(peer, carry):
        peer_zh, peer_zl = lax.shift_right_logical(peer, 1), peer & 1
        slot = 2 * ((y * 4 + peer_zh) * 2 + core)
        wanted = [
            slot_ref[slot] * 8 + peer_zl * 4 + x,
            slot_ref[slot + 1] * 8 + peer_zl * 4 + x,
            slot_ref[slot + peer_zl] * 8 + 2 * x,
            slot_ref[slot + peer_zl] * 8 + 2 * x + 1,
        ]
        p = jnp.concatenate([order_ref[pl.ds(row, 1), :] for row in wanted], axis=1)
        gy, gzh, gcore, gzl, gx = place(lax.shift_right_logical(p, 8))
        here = (gzh == zh) & (gzl == zl)
        holder = jnp.where(here, ((gcore ^ core) * 4 + gx) * 4 + gy, -1)
        chosen = (member == (p & (PART - 1))).astype(jnp.bfloat16)
        holder = jnp.broadcast_to(holder, (2 * DIM, 2 * PART))
        found = jnp.zeros((2 * DIM, 2 * PART), jnp.float32)
        for source in range(2):
            table = (other_ref if source else mine_ref)[...].reshape(XY * 2 * DIM, PART)
            taken = jnp.dot(table, chosen, preferred_element_type=jnp.float32)
            for dev in range(XY):
                rows = taken[dev * 2 * DIM : (dev + 1) * 2 * DIM]
                found = jnp.where(holder == source * XY + dev, rows, found)
        found = found.astype(jnp.bfloat16)
        out_ref[peer, : 2 * DIM, :] = found[:, :PART]
        out_ref[peer, 2 * DIM :, :] = found[:, PART:]
        return carry

    lax.fori_loop(0, ZS, one_peer, 0, unroll=4)


def pack_kernel(parts_ref, inc_ref, rows_ref, cols_ref):
    total = parts_ref[0].astype(jnp.float32)
    for peer in range(1, ZS):
        total += parts_ref[peer].astype(jnp.float32)
    total = total.astype(jnp.bfloat16)
    inc = inc_ref[...]
    for dev in range(XY):
        rows_ref[dev, :COLS, :] = inc
        rows_ref[dev, COLS:, :] = total[: 2 * DIM]
    for dev in range(ZS):
        cols_ref[dev] = total[2 * DIM :]


def three_terms(value):
    first = value.astype(jnp.bfloat16).astype(jnp.float32)
    second = (value - first).astype(jnp.bfloat16).astype(jnp.float32)
    return first, second, value - first - second


def features(high, low, left, extra):
    full = high.astype(jnp.float32) + low.astype(jnp.float32)
    norm = extra - 0.5 * jnp.sum(full * full, axis=0, keepdims=True)
    first, second, third = three_terms(norm)
    row = lax.broadcasted_iota(jnp.int32, high.shape, 0)
    base = 0 if left else 3
    tail = jnp.where((row >= 3 - base) & (row < 6 - base), 1.0, 0.0)
    tail = jnp.where(row == base, first, tail)
    tail = jnp.where(row == base + 1, second, tail)
    tail = jnp.where(row == base + 2, third, tail)
    tail = tail.astype(jnp.bfloat16)
    pieces = [high, low, high, low, tail] if left else [high, high, low, low, tail]
    return jnp.concatenate(pieces, axis=0)


FEATURES = 5 * DIM
TILE = 512
DEPTH = 1
EACH = 2


def exponents(left, right_ref, tile):
    return lax.dot_general(
        left,
        right_ref[:, tile * TILE : (tile + 1) * TILE],
        (((0,), (0,)), ((), ())),
        preferred_element_type=jnp.float32,
    )


def add_rows(source, right_ref, out_ref):
    tiles = ZS * PART // TILE

    def step(index, carry):
        work = []
        for k in range(EACH):
            values, left = [], []
            for j in range(2):
                block = source[(index * EACH + k) * 2 + j]
                values.append(block[:COLS])
                left.append(features(block[COLS : COLS + DIM], block[COLS + DIM :], True, 0.0))
            values = jnp.concatenate(values, axis=1)
            left = jnp.concatenate(left, axis=1)
            work += [(values, left, tile) for tile in range(tiles)]
        ahead = [exponents(left, right_ref, tile) for _, left, tile in work[:DEPTH]]
        for at, (values, _, tile) in enumerate(work):
            if at + DEPTH < len(work):
                ahead.append(exponents(work[at + DEPTH][1], right_ref, work[at + DEPTH][2]))
            entries = jnp.exp2(ahead[at]).astype(jnp.bfloat16)
            part = jnp.dot(values, entries, preferred_element_type=jnp.float32)
            for k in range(TILE // PART):
                out_ref[tile * (TILE // PART) + k] += part[:, k * PART : (k + 1) * PART]
        return carry

    lax.fori_loop(0, XY // (2 * EACH), step, 0)


def first_kernel(flat_ref, mine_ref, cols_ref, out_ref, right_ref):
    y, zh, core, zl, x = place(flat_ref[0])
    for peer in range(ZS):
        right_ref[:, peer * PART : (peer + 1) * PART] = features(
            cols_ref[peer, :DIM], cols_ref[peer, DIM:], False, LOG2AMP
        )
    out_ref[...] = jnp.zeros_like(out_ref)
    add_rows(mine_ref, right_ref, out_ref)

    @pl.when(lax.shift_right_logical(x, 1) == zl)
    def _():
        for j in range(2):
            dev = (2 * (x & 1) + j) * 4 + y
            for s in range(2):
                noise = noise_var * mine_ref[dev, 0:COLS, s * LANES : (s + 1) * LANES].astype(jnp.float32)
                out_ref[zh * 2 + s, :, j * LANES : (j + 1) * LANES] += noise


def second_kernel(flat_ref, other_ref, right_ref, so_far_ref, out_ref, own_ref, sum_ref):
    _, zh, _, zl, _ = place(flat_ref[0])
    sum_ref[...] = so_far_ref[...]
    add_rows(other_ref, right_ref, sum_ref)
    out_ref[...] = sum_ref[...].astype(jnp.bfloat16)
    own_ref[...] = sum_ref[zh * 2 + zl]


def end_kernel(flat_ref, own_ref, parts_ref, res_ref, out_ref):
    _, zh, _, zl, x = place(flat_ref[0])
    change = own_ref[...]
    for peer in range(ZS):
        change += jnp.where(peer == zh * 2 + zl, 0.0, parts_ref[peer].astype(jnp.float32))
    for s in range(2):
        for k in range(4):

            @pl.when((zl == s) & (x == k))
            def _(s=s, k=k):
                out_ref[...] = res_ref[:, s, k * PART : (k + 1) * PART] - change


def exchange(pieces, axes):
    return lax.all_to_all(pieces, axes, split_axis=0, concat_axis=0, tiled=True)


def swap_core(value):
    return lax.ppermute(value, "core", [(0, 1), (1, 0)])


def call(kernel, shapes, scalars, arrays, scratch=()):
    return pl.pallas_call(
        kernel,
        out_shape=shapes,
        in_specs=[SM] * len(scalars) + [VM] * len(arrays),
        out_specs=jax.tree.map(lambda _: VM, shapes),
        scratch_shapes=scratch,
        compiler_params=pltpu.CompilerParams(vmem_limit_bytes=KERNEL_VMEM),
    )(*scalars, *[pltpu.with_memory_space_constraint(a, pltpu.VMEM) for a in arrays])


def per_device(points, lengthscales, point_order, block_slot, block_inverses, residual):
    f32, bf16, shape, whole = jnp.float32, jnp.bfloat16, pltpu.VMEM, jax.ShapeDtypeStruct
    flat = lax.axis_index(AXES).astype(jnp.int32)[None]
    start = call(start_kernel, shape((XY, 2 * DIM, PART), bf16), [lengthscales], [points])
    mine = exchange(start, ("x", "y"))
    other = swap_core(mine)
    increments, flat_inc = call(
        solve_kernel,
        (whole((COLS, 2, LANES), bf16), shape((COLS, PART), bf16)),
        [],
        [block_inverses, residual],
    )
    picked = call(
        pick_kernel,
        shape((ZS, 4 * DIM, PART), bf16),
        [flat, block_slot],
        [point_order.reshape(-1, LANES), mine, other, flat_inc],
    )
    row_pack, col_pack = call(
        pack_kernel,
        (shape((XY, COLS + 2 * DIM, PART), bf16), shape((ZS, 2 * DIM, PART), bf16)),
        [],
        [exchange(picked, ("zh", "zl")), flat_inc],
    )
    rows_mine = exchange(row_pack, ("x", "y"))
    rows_other = swap_core(rows_mine)
    cols = exchange(col_pack, ("zh", "zl"))
    partial, right = call(
        first_kernel,
        (shape((ZS, COLS, PART), f32), shape((FEATURES, ZS * PART), bf16)),
        [flat],
        [rows_mine, cols],
    )
    partial, own = call(
        second_kernel,
        (shape((ZS, COLS, PART), bf16), shape((COLS, PART), f32)),
        [flat],
        [rows_other, right, partial],
        [pltpu.VMEM((ZS, COLS, PART), f32)],
    )
    parts = exchange(partial, ("zh", "zl"))
    return increments, call(end_kernel, whole((COLS, PART), f32), [flat], [own, parts, residual])


def solution(mesh):
    fine = Mesh(np.asarray(mesh.devices).reshape(SIZES), AXES)
    row, blk = ("y", "zh", "core"), ("zl", "x")
    return jax.shard_map(
        per_device,
        mesh=fine,
        in_specs=(P(None, AXES), P(), P(), P(), P(row, blk, None), P(None, row, None)),
        out_specs=(P(None, row, blk), P(None, AXES)),
        check_vma=False,
    )
```

```python
import math

import jax
import jax.numpy as jnp
import numpy as np
from jax import lax
from jax.experimental import pallas as pl
from jax.experimental.pallas import tpu as pltpu
from jax.sharding import Mesh
from jax.sharding import PartitionSpec as P

damping = 0.5
amplitude = 0.3
noise_var = 0.25

AXES = ("y", "zh", "core", "zl", "x")
SIZES = (4, 4, 2, 2, 4)
DIM = 16
COLS = 64
PART = 256
BS = 1024
NBLK = 64
LANES = 128
BLK = 8
NEAR = 4
PLANE = 16
KERNEL_VMEM = 16 << 20
LOG2E = math.log2(math.e)
LOG2AMP = math.log2(amplitude)

VM = pl.BlockSpec(memory_space=pltpu.VMEM)
SM = pl.BlockSpec(memory_space=pltpu.SMEM)


def place(f):
    return (
        lax.shift_right_logical(f, 6),
        lax.shift_right_logical(f, 4) & 3,
        lax.shift_right_logical(f, 3) & 1,
        lax.shift_right_logical(f, 2) & 1,
        f & 3,
    )


def solve_kernel(inv_ref, res_ref, inc_ref, flat_ref):
    for s in range(2):
        low = res_ref[:, s, :].astype(jnp.bfloat16)
        solved = lax.dot_general(
            low, inv_ref[s], (((1,), (1,)), ((), ())), preferred_element_type=jnp.float32
        )
        inc = (damping * solved).astype(jnp.bfloat16)
        inc_ref[:, s, :] = inc
        flat_ref[:, s * LANES : (s + 1) * LANES] = inc


def start_kernel(scale_ref, points_ref, out_ref):
    scale = jnp.concatenate([jnp.full((1, PART), scale_ref[d], jnp.float32) for d in range(DIM)], axis=0)
    own = (points_ref[...] - 0.5) * (math.sqrt(LOG2E) / scale)
    high = own.astype(jnp.bfloat16)
    low = (own - high.astype(jnp.float32)).astype(jnp.bfloat16)
    for dev in range(PLANE):
        out_ref[dev, :DIM, :] = high
        out_ref[dev, DIM:, :] = low


def pick_kernel(flat_ref, slot_ref, order_ref, mine_ref, other_ref, _, out_ref):
    y, zh, core, zl, x = place(flat_ref[0])
    member = lax.broadcasted_iota(jnp.int32, (PART, 2 * PART), 0)

    def two_peers(pair, carry):
        slot = 2 * ((y * 4 + pair) * 2 + core)
        wanted = [slot_ref[slot + s] * 8 + peer_zl * 4 + x for peer_zl in range(2) for s in range(2)]
        p = jnp.concatenate([order_ref[pl.ds(row, 1), :] for row in wanted], axis=1)
        gy, gzh, gcore, gzl, gx = place(lax.shift_right_logical(p, 8))
        here = (gzh == zh) & (gzl == zl)
        holder = jnp.where(here, ((gcore ^ core) * 4 + gy) * 4 + gx, -1)
        chosen = (member == (p & (PART - 1))).astype(jnp.bfloat16)
        holder = jnp.broadcast_to(holder, (2 * DIM, 2 * PART))
        found = jnp.zeros((2 * DIM, 2 * PART), jnp.float32)
        for source in range(2):
            table = (other_ref if source else mine_ref)[...].reshape(PLANE * 2 * DIM, PART)
            taken = jnp.dot(table, chosen, preferred_element_type=jnp.float32)
            for dev in range(PLANE):
                rows = taken[dev * 2 * DIM : (dev + 1) * 2 * DIM]
                found = jnp.where(holder == source * PLANE + dev, rows, found)
        found = found.astype(jnp.bfloat16)
        out_ref[2 * pair] = found[:, :PART]
        out_ref[2 * pair + 1] = found[:, PART:]
        return carry

    lax.fori_loop(0, BLK // 2, two_peers, 0, unroll=4)


def pack_kernel(parts_ref, inc_ref, rows_ref, cols_ref):
    total = parts_ref[0].astype(jnp.float32)
    for peer in range(1, BLK):
        total += parts_ref[peer].astype(jnp.float32)
    total = total.astype(jnp.bfloat16)
    inc = inc_ref[...]
    for dev in range(NEAR):
        rows_ref[dev, :COLS, :] = inc
        rows_ref[dev, COLS:, :] = total
    for dev in range(BLK):
        cols_ref[dev] = total


def three_terms(value):
    first = value.astype(jnp.bfloat16).astype(jnp.float32)
    second = (value - first).astype(jnp.bfloat16).astype(jnp.float32)
    return first, second, value - first - second


def features(high, low, left, extra):
    full = high.astype(jnp.float32) + low.astype(jnp.float32)
    norm = extra - 0.5 * jnp.sum(full * full, axis=0, keepdims=True)
    first, second, third = three_terms(norm)
    row = lax.broadcasted_iota(jnp.int32, high.shape, 0)
    base = 0 if left else 3
    tail = jnp.where((row >= 3 - base) & (row < 6 - base), 1.0, 0.0)
    tail = jnp.where(row == base, first, tail)
    tail = jnp.where(row == base + 1, second, tail)
    tail = jnp.where(row == base + 2, third, tail)
    tail = tail.astype(jnp.bfloat16)
    pieces = [high, low, high, low, tail] if left else [high, high, low, low, tail]
    return jnp.concatenate(pieces, axis=0)


FEATURES = 5 * DIM
TILE = 512
DEPTH = 1


def exponents(left, right_ref, tile):
    return lax.dot_general(
        left,
        right_ref[:, tile * TILE : (tile + 1) * TILE],
        (((0,), (0,)), ((), ())),
        preferred_element_type=jnp.float32,
    )


def add_rows(sources, right_ref, out_ref):
    work = []
    for source in sources:
        for pair in range(NEAR // 2):
            values, left = [], []
            for j in range(2):
                block = source[pair * 2 + j]
                values.append(block[:COLS])
                left.append(features(block[COLS : COLS + DIM], block[COLS + DIM :], True, 0.0))
            values = jnp.concatenate(values, axis=1)
            left = jnp.concatenate(left, axis=1)
            work += [(values, left, tile) for tile in range(BLK * PART // TILE)]
    ahead = [exponents(left, right_ref, tile) for _, left, tile in work[:DEPTH]]
    for at, (values, _, tile) in enumerate(work):
        if at + DEPTH < len(work):
            ahead.append(exponents(work[at + DEPTH][1], right_ref, work[at + DEPTH][2]))
        entries = jnp.exp2(ahead[at]).astype(jnp.bfloat16)
        part = jnp.dot(values, entries, preferred_element_type=jnp.float32)
        for k in range(TILE // PART):
            out_ref[tile * (TILE // PART) + k] += part[:, k * PART : (k + 1) * PART]


def first_kernel(flat_ref, mine_ref, cols_ref, out_ref, right_ref):
    _, zh, _, zl, x = place(flat_ref[0])
    for peer in range(BLK):
        s, first = peer // 4, 2 * (peer % 4)
        block = jnp.concatenate(
            [cols_ref[first + j, :, s * LANES : (s + 1) * LANES] for j in range(2)], axis=1
        )
        right_ref[:, peer * PART : (peer + 1) * PART] = features(block[:DIM], block[DIM:], False, LOG2AMP)
    out_ref[...] = jnp.zeros_like(out_ref)
    add_rows([mine_ref], right_ref, out_ref)
    inc = noise_var * mine_ref[zh, :COLS, :].astype(jnp.float32)
    for half in range(2):

        @pl.when((x & 1) == half)
        def _():
            for s in range(2):
                at = s * 4 + zl * 2 + lax.shift_right_logical(x, 1)
                out_ref[at, :, half * LANES : (half + 1) * LANES] += inc[:, s * LANES : (s + 1) * LANES]


def second_kernel(right_ref, so_far_ref, a_ref, b_ref, c_ref, out_ref):
    out_ref[...] = so_far_ref[...]
    add_rows([a_ref, b_ref, c_ref], right_ref, out_ref)


def third_kernel(flat_ref, right_ref, so_far_ref, a_ref, b_ref, c_ref, d_ref, out_ref, own_ref, sum_ref):
    _, _, _, zl, x = place(flat_ref[0])
    sum_ref[...] = so_far_ref[...]
    add_rows([a_ref, b_ref, c_ref, d_ref], right_ref, sum_ref)
    out_ref[...] = sum_ref[...].astype(jnp.bfloat16)
    own_ref[...] = sum_ref[zl * 4 + x]


def end_kernel(flat_ref, own_ref, parts_ref, res_ref, out_ref):
    _, _, _, zl, x = place(flat_ref[0])
    change = own_ref[...]
    for peer in range(BLK):
        change += jnp.where(peer == zl * 4 + x, 0.0, parts_ref[peer].astype(jnp.float32))
    for s in range(2):
        for k in range(4):

            @pl.when((zl == s) & (x == k))
            def _(s=s, k=k):
                out_ref[...] = res_ref[:, s, k * PART : (k + 1) * PART] - change


def exchange(pieces, axes):
    return lax.all_to_all(pieces, axes, split_axis=0, concat_axis=0, tiled=True)


def swap_core(value):
    return lax.ppermute(value, "core", [(0, 1), (1, 0)])


def call(kernel, shapes, scalars, arrays, scratch=(), fetched=()):
    return pl.pallas_call(
        kernel,
        out_shape=shapes,
        in_specs=[SM] * len(scalars) + [VM] * (len(fetched) + len(arrays)),
        out_specs=jax.tree.map(lambda _: VM, shapes),
        scratch_shapes=scratch,
        compiler_params=pltpu.CompilerParams(vmem_limit_bytes=KERNEL_VMEM),
    )(
        *[pltpu.with_memory_space_constraint(a, pltpu.HBM) for a in [*scalars, *fetched]],
        *[pltpu.with_memory_space_constraint(a, pltpu.VMEM) for a in arrays],
    )


def per_device(points, lengthscales, point_order, block_slot, block_inverses, residual):
    f32, bf16, shape, whole = jnp.float32, jnp.bfloat16, pltpu.VMEM, jax.ShapeDtypeStruct
    flat = lax.axis_index(AXES).astype(jnp.int32)[None]
    start = call(
        start_kernel,
        shape((PLANE, 2 * DIM, PART), bf16),
        [lengthscales],
        [],
        fetched=[points],
    )
    mine = exchange(start, ("y", "x"))
    other = swap_core(mine)
    increments, flat_inc = call(
        solve_kernel,
        (whole((COLS, 2, LANES), bf16), shape((COLS, PART), bf16)),
        [],
        [residual],
        fetched=[block_inverses],
    )
    picked = call(
        pick_kernel,
        shape((BLK, 2 * DIM, PART), bf16),
        [flat, block_slot],
        [point_order.reshape(-1, LANES), mine, other, flat_inc],
    )
    packed, cols = call(
        pack_kernel,
        (shape((NEAR, COLS + 2 * DIM, PART), bf16), shape((BLK, 2 * DIM, PART), bf16)),
        [],
        [exchange(picked, ("zh", "zl")), flat_inc],
    )
    rows = exchange(packed, "zh")
    moved = [lax.ppermute(rows, "y", [(k, (k + shift) % 4) for k in range(4)]) for shift in (1, 3, 2)]
    cols = exchange(cols, ("zl", "x"))
    swapped = [swap_core(value) for value in [rows, *moved]]
    partial, right = call(
        first_kernel,
        (shape((BLK, COLS, PART), f32), shape((FEATURES, BLK * PART), bf16)),
        [flat],
        [rows, cols],
    )
    partial = call(second_kernel, shape((BLK, COLS, PART), f32), [], [right, partial, *moved])
    partial, own = call(
        third_kernel,
        (shape((BLK, COLS, PART), bf16), shape((COLS, PART), f32)),
        [flat],
        [right, partial, *swapped],
        [pltpu.VMEM((BLK, COLS, PART), f32)],
    )
    parts = exchange(partial, ("zl", "x"))
    return increments, call(end_kernel, whole((COLS, PART), f32), [flat], [own, parts, residual])


def solution(mesh):
    fine = Mesh(np.asarray(mesh.devices).reshape(SIZES), AXES)
    row, blk = ("y", "zh", "core"), ("zl", "x")
    return jax.shard_map(
        per_device,
        mesh=fine,
        in_specs=(P(None, AXES), P(), P(), P(), P(row, blk, None), P(None, row, None)),
        out_specs=(P(None, row, blk), P(None, AXES)),
        check_vma=False,
    )
```

```python
import math

import jax
import jax.numpy as jnp
import numpy as np
from jax import lax
from jax.experimental import pallas as pl
from jax.experimental.pallas import tpu as pltpu
from jax.sharding import Mesh
from jax.sharding import PartitionSpec as P

damping = 0.5
amplitude = 0.3
noise_var = 0.25

AXES = ("y", "zh", "core", "zl", "x")
SIZES = (4, 4, 2, 2, 4)
DIM = 16
COLS = 64
PART = 256
BS = 1024
NBLK = 64
LANES = 128
BLK = 8
NEAR = 4
PLANE = 16
KERNEL_VMEM = 16 << 20
LOG2E = math.log2(math.e)
LOG2AMP = math.log2(amplitude)

VM = pl.BlockSpec(memory_space=pltpu.VMEM)
SM = pl.BlockSpec(memory_space=pltpu.SMEM)


def place(f):
    return (
        lax.shift_right_logical(f, 6),
        lax.shift_right_logical(f, 4) & 3,
        lax.shift_right_logical(f, 3) & 1,
        lax.shift_right_logical(f, 2) & 1,
        f & 3,
    )


def solve_kernel(inv_ref, res_ref, inc_ref, flat_ref):
    found = []
    for s in range(2):
        low = [res_ref[pl.ds(2 * j + s, COLS, stride=16), :].astype(jnp.bfloat16) for j in range(BS // LANES)]
        solved = lax.dot_general(
            jnp.concatenate(low, axis=1),
            inv_ref[s],
            (((1,), (1,)), ((), ())),
            preferred_element_type=jnp.float32,
        )
        inc = (damping * solved).astype(jnp.bfloat16)
        flat_ref[:, s * LANES : (s + 1) * LANES] = inc
        found.append(inc)
    for s in range(2):
        inc_ref[:, s, :] = found[s]


def start_kernel(scale_ref, points_ref, out_ref):
    scale = jnp.concatenate([jnp.full((1, PART), scale_ref[d], jnp.float32) for d in range(DIM)], axis=0)
    own = (points_ref[...] - 0.5) * (math.sqrt(LOG2E) / scale)
    high = own.astype(jnp.bfloat16)
    low = (own - high.astype(jnp.float32)).astype(jnp.bfloat16)
    for dev in range(PLANE):
        out_ref[dev, :DIM, :] = high
        out_ref[dev, DIM:, :] = low


def pick_kernel(flat_ref, slot_ref, order_ref, mine_ref, other_ref, _, out_ref):
    y, zh, core, zl, x = place(flat_ref[0])
    member = lax.broadcasted_iota(jnp.int32, (PART, 2 * PART), 0)

    def two_peers(pair, carry):
        slot = 2 * ((y * 4 + pair) * 2 + core)
        wanted = [slot_ref[slot + s] * 8 + peer_zl * 4 + x for peer_zl in range(2) for s in range(2)]
        p = jnp.concatenate([order_ref[pl.ds(row, 1), :] for row in wanted], axis=1)
        gy, gzh, gcore, gzl, gx = place(lax.shift_right_logical(p, 8))
        here = (gzh == zh) & (gzl == zl)
        holder = jnp.where(here, ((gcore ^ core) * 4 + gy) * 4 + gx, -1)
        chosen = (member == (p & (PART - 1))).astype(jnp.bfloat16)
        holder = jnp.broadcast_to(holder, (2 * DIM, 2 * PART))
        found = jnp.zeros((2 * DIM, 2 * PART), jnp.float32)
        for source in range(2):
            table = (other_ref if source else mine_ref)[...].reshape(PLANE * 2 * DIM, PART)
            taken = jnp.dot(table, chosen, preferred_element_type=jnp.float32)
            for dev in range(PLANE):
                rows = taken[dev * 2 * DIM : (dev + 1) * 2 * DIM]
                found = jnp.where(holder == source * PLANE + dev, rows, found)
        found = found.astype(jnp.bfloat16)
        out_ref[2 * pair] = found[:, :PART]
        out_ref[2 * pair + 1] = found[:, PART:]
        return carry

    lax.fori_loop(0, BLK // 2, two_peers, 0, unroll=4)


def pack_kernel(parts_ref, inc_ref, rows_ref, cols_ref):
    total = parts_ref[0].astype(jnp.float32)
    for peer in range(1, BLK):
        total += parts_ref[peer].astype(jnp.float32)
    total = total.astype(jnp.bfloat16)
    inc = inc_ref[...]
    for dev in range(NEAR):
        rows_ref[dev, :COLS, :] = inc
        rows_ref[dev, COLS:, :] = total
    for dev in range(BLK):
        cols_ref[dev] = total


def three_terms(value):
    first = value.astype(jnp.bfloat16).astype(jnp.float32)
    second = (value - first).astype(jnp.bfloat16).astype(jnp.float32)
    return first, second, value - first - second


def features(high, low, left, extra):
    full = high.astype(jnp.float32) + low.astype(jnp.float32)
    norm = extra - 0.5 * jnp.sum(full * full, axis=0, keepdims=True)
    first, second, third = three_terms(norm)
    row = lax.broadcasted_iota(jnp.int32, high.shape, 0)
    base = 0 if left else 3
    tail = jnp.where((row >= 3 - base) & (row < 6 - base), 1.0, 0.0)
    tail = jnp.where(row == base, first, tail)
    tail = jnp.where(row == base + 1, second, tail)
    tail = jnp.where(row == base + 2, third, tail)
    tail = tail.astype(jnp.bfloat16)
    pieces = [high, low, high, low, tail] if left else [high, high, low, low, tail]
    return jnp.concatenate(pieces, axis=0)


FEATURES = 5 * DIM
TILE = 512
DEPTH = 1


def exponents(left, right_ref, tile):
    return lax.dot_general(
        left,
        right_ref[:, tile * TILE : (tile + 1) * TILE],
        (((0,), (0,)), ((), ())),
        preferred_element_type=jnp.float32,
    )


def add_rows(sources, right_ref, out_ref):
    work = []
    for source in sources:
        for pair in range(NEAR // 2):
            values, left = [], []
            for j in range(2):
                block = source[pair * 2 + j]
                values.append(block[:COLS])
                left.append(features(block[COLS : COLS + DIM], block[COLS + DIM :], True, 0.0))
            values = jnp.concatenate(values, axis=1)
            left = jnp.concatenate(left, axis=1)
            work += [(values, left, tile) for tile in range(BLK * PART // TILE)]
    ahead = [exponents(left, right_ref, tile) for _, left, tile in work[:DEPTH]]
    for at, (values, _, tile) in enumerate(work):
        if at + DEPTH < len(work):
            ahead.append(exponents(work[at + DEPTH][1], right_ref, work[at + DEPTH][2]))
        entries = jnp.exp2(ahead[at]).astype(jnp.bfloat16)
        part = jnp.dot(values, entries, preferred_element_type=jnp.float32)
        for k in range(TILE // PART):
            out_ref[tile * (TILE // PART) + k] += part[:, k * PART : (k + 1) * PART]


def first_kernel(flat_ref, mine_ref, cols_ref, out_ref, right_ref):
    _, zh, _, zl, x = place(flat_ref[0])
    for peer in range(BLK):
        s, first = peer // 4, 2 * (peer % 4)
        block = jnp.concatenate(
            [cols_ref[first + j, :, s * LANES : (s + 1) * LANES] for j in range(2)], axis=1
        )
        right_ref[:, peer * PART : (peer + 1) * PART] = features(block[:DIM], block[DIM:], False, LOG2AMP)
    out_ref[...] = jnp.zeros_like(out_ref)
    add_rows([mine_ref], right_ref, out_ref)
    inc = noise_var * mine_ref[zh, :COLS, :].astype(jnp.float32)
    for half in range(2):

        @pl.when((x & 1) == half)
        def _():
            for s in range(2):
                at = s * 4 + zl * 2 + lax.shift_right_logical(x, 1)
                out_ref[at, :, half * LANES : (half + 1) * LANES] += inc[:, s * LANES : (s + 1) * LANES]


def second_kernel(right_ref, so_far_ref, a_ref, b_ref, c_ref, out_ref):
    out_ref[...] = so_far_ref[...]
    add_rows([a_ref, b_ref, c_ref], right_ref, out_ref)


def third_kernel(flat_ref, right_ref, so_far_ref, a_ref, b_ref, c_ref, d_ref, out_ref, own_ref, sum_ref):
    _, _, _, zl, x = place(flat_ref[0])
    sum_ref[...] = so_far_ref[...]
    add_rows([a_ref, b_ref, c_ref, d_ref], right_ref, sum_ref)
    out_ref[...] = sum_ref[...].astype(jnp.bfloat16)
    own_ref[...] = sum_ref[zl * 4 + x]


def end_kernel(flat_ref, own_ref, parts_ref, res_ref, out_ref):
    _, _, _, zl, x = place(flat_ref[0])
    change = own_ref[...]
    for peer in range(BLK):
        change += jnp.where(peer == zl * 4 + x, 0.0, parts_ref[peer].astype(jnp.float32))
    for k in range(2):
        old = res_ref[pl.ds(4 * x + 2 * k + zl, COLS, stride=16), :]
        out_ref[:, k * LANES : (k + 1) * LANES] = old - change[:, k * LANES : (k + 1) * LANES]


def exchange(pieces, axes):
    return lax.all_to_all(pieces, axes, split_axis=0, concat_axis=0, tiled=True)


def swap_core(value):
    return lax.ppermute(value, "core", [(0, 1), (1, 0)])


def call(kernel, shapes, scalars, arrays, scratch=(), fetched=()):
    return pl.pallas_call(
        kernel,
        out_shape=shapes,
        in_specs=[SM] * len(scalars) + [VM] * (len(fetched) + len(arrays)),
        out_specs=jax.tree.map(lambda _: VM, shapes),
        scratch_shapes=scratch,
        compiler_params=pltpu.CompilerParams(vmem_limit_bytes=KERNEL_VMEM),
    )(
        *[pltpu.with_memory_space_constraint(a, pltpu.HBM) for a in [*scalars, *fetched]],
        *[pltpu.with_memory_space_constraint(a, pltpu.VMEM) for a in arrays],
    )


def per_device(points, lengthscales, point_order, block_slot, block_inverses, residual):
    f32, bf16, shape, whole = jnp.float32, jnp.bfloat16, pltpu.VMEM, jax.ShapeDtypeStruct
    flat = lax.axis_index(AXES).astype(jnp.int32)[None]
    rows = residual.reshape(COLS, 2, BS // LANES, LANES).transpose(0, 2, 1, 3).reshape(-1, LANES)
    start = call(
        start_kernel,
        shape((PLANE, 2 * DIM, PART), bf16),
        [lengthscales],
        [],
        fetched=[points],
    )
    mine = exchange(start, ("y", "x"))
    other = swap_core(mine)
    increments, flat_inc = call(
        solve_kernel,
        (whole((COLS, 2, LANES), bf16), shape((COLS, PART), bf16)),
        [],
        [rows],
        fetched=[block_inverses],
    )
    picked = call(
        pick_kernel,
        shape((BLK, 2 * DIM, PART), bf16),
        [flat, block_slot],
        [point_order.reshape(-1, LANES), mine, other, flat_inc],
    )
    packed, cols = call(
        pack_kernel,
        (shape((NEAR, COLS + 2 * DIM, PART), bf16), shape((BLK, 2 * DIM, PART), bf16)),
        [],
        [exchange(picked, ("zh", "zl")), flat_inc],
    )
    taken = exchange(packed, "zh")
    moved = [lax.ppermute(taken, "y", [(k, (k + shift) % 4) for k in range(4)]) for shift in (1, 3, 2)]
    cols = exchange(cols, ("zl", "x"))
    swapped = [swap_core(value) for value in [taken, *moved]]
    partial, right = call(
        first_kernel,
        (shape((BLK, COLS, PART), f32), shape((FEATURES, BLK * PART), bf16)),
        [flat],
        [taken, cols],
    )
    partial = call(second_kernel, shape((BLK, COLS, PART), f32), [], [right, partial, *moved])
    partial, own = call(
        third_kernel,
        (shape((BLK, COLS, PART), bf16), shape((COLS, PART), f32)),
        [flat],
        [right, partial, *swapped],
        [pltpu.VMEM((BLK, COLS, PART), f32)],
    )
    parts = exchange(partial, ("zl", "x"))
    return increments, call(end_kernel, whole((COLS, PART), f32), [flat], [own, parts, rows])


def solution(mesh):
    fine = Mesh(np.asarray(mesh.devices).reshape(SIZES), AXES)
    row, blk = ("y", "zh", "core"), ("zl", "x")
    return jax.shard_map(
        per_device,
        mesh=fine,
        in_specs=(P(None, AXES), P(), P(), P(), P(row, blk, None), P(None, row, None)),
        out_specs=(P(None, row, blk), P(None, AXES)),
        check_vma=False,
    )
```

```python
import math

import jax
import jax.numpy as jnp
import numpy as np
from jax import lax
from jax.experimental import pallas as pl
from jax.experimental.pallas import tpu as pltpu
from jax.sharding import Mesh
from jax.sharding import PartitionSpec as P

damping = 0.5
amplitude = 0.3
noise_var = 0.25

AXES = ("y", "zh", "core", "zl", "x")
SIZES = (4, 4, 2, 2, 4)
DIM = 16
COLS = 64
PART = 256
BS = 1024
NBLK = 64
LANES = 128
BLK = 8
NEAR = 4
PLANE = 16
KERNEL_VMEM = 16 << 20
LOG2E = math.log2(math.e)
LOG2AMP = math.log2(amplitude)

VM = pl.BlockSpec(memory_space=pltpu.VMEM)
SM = pl.BlockSpec(memory_space=pltpu.SMEM)
ANY = pl.BlockSpec(memory_space=pl.ANY)


def place(f):
    return (
        lax.shift_right_logical(f, 6),
        lax.shift_right_logical(f, 4) & 3,
        lax.shift_right_logical(f, 3) & 1,
        lax.shift_right_logical(f, 2) & 1,
        f & 3,
    )


def solve_kernel(inv_ref, res_ref, inc_ref, flat_ref, held, arrived):
    copies = []
    for s in range(2):
        for q in range(4):
            rows = pl.ds(q * 32, 32)
            copy = pltpu.make_async_copy(inv_ref.at[s, rows, :], held.at[s, rows, :], arrived.at[s * 4 + q])
            copy.start()
            copies.append(copy)
    low = []
    for s in range(2):
        parts = [res_ref[pl.ds(2 * j + s, COLS, stride=16), :].astype(jnp.bfloat16) for j in range(BS // LANES)]
        low.append(jnp.concatenate(parts, axis=1))
    for copy in copies:
        copy.wait()
    for s in range(2):
        solved = lax.dot_general(
            low[s], held[s], (((1,), (1,)), ((), ())), preferred_element_type=jnp.float32
        )
        inc = (damping * solved).astype(jnp.bfloat16)
        inc_ref[:, s, :] = inc
        flat_ref[:, s * LANES : (s + 1) * LANES] = inc


def start_kernel(scale_ref, points_ref, out_ref):
    scale = jnp.concatenate([jnp.full((1, PART), scale_ref[d], jnp.float32) for d in range(DIM)], axis=0)
    own = (points_ref[...] - 0.5) * (math.sqrt(LOG2E) / scale)
    high = own.astype(jnp.bfloat16)
    low = (own - high.astype(jnp.float32)).astype(jnp.bfloat16)
    for dev in range(PLANE):
        out_ref[dev, :DIM, :] = high
        out_ref[dev, DIM:, :] = low


def pick_kernel(flat_ref, slot_ref, order_ref, mine_ref, other_ref, _, out_ref):
    y, zh, core, zl, x = place(flat_ref[0])
    member = lax.broadcasted_iota(jnp.int32, (PART, 2 * PART), 0)

    def two_peers(pair, carry):
        slot = 2 * ((y * 4 + pair) * 2 + core)
        wanted = [slot_ref[slot + s] * 8 + peer_zl * 4 + x for peer_zl in range(2) for s in range(2)]
        p = jnp.concatenate([order_ref[pl.ds(row, 1), :] for row in wanted], axis=1)
        gy, gzh, gcore, gzl, gx = place(lax.shift_right_logical(p, 8))
        here = (gzh == zh) & (gzl == zl)
        holder = jnp.where(here, ((gcore ^ core) * 4 + gy) * 4 + gx, -1)
        chosen = (member == (p & (PART - 1))).astype(jnp.bfloat16)
        holder = jnp.broadcast_to(holder, (2 * DIM, 2 * PART))
        found = jnp.zeros((2 * DIM, 2 * PART), jnp.float32)
        for source in range(2):
            table = (other_ref if source else mine_ref)[...].reshape(PLANE * 2 * DIM, PART)
            taken = jnp.dot(table, chosen, preferred_element_type=jnp.float32)
            for dev in range(PLANE):
                rows = taken[dev * 2 * DIM : (dev + 1) * 2 * DIM]
                found = jnp.where(holder == source * PLANE + dev, rows, found)
        found = found.astype(jnp.bfloat16)
        out_ref[2 * pair] = found[:, :PART]
        out_ref[2 * pair + 1] = found[:, PART:]
        return carry

    lax.fori_loop(0, BLK // 2, two_peers, 0, unroll=4)


def pack_kernel(parts_ref, inc_ref, rows_ref, cols_ref):
    total = parts_ref[0].astype(jnp.float32)
    for peer in range(1, BLK):
        total += parts_ref[peer].astype(jnp.float32)
    total = total.astype(jnp.bfloat16)
    inc = inc_ref[...]
    for dev in range(NEAR):
        rows_ref[dev, :COLS, :] = inc
        rows_ref[dev, COLS:, :] = total
    for dev in range(BLK):
        cols_ref[dev] = total


def three_terms(value):
    first = value.astype(jnp.bfloat16).astype(jnp.float32)
    second = (value - first).astype(jnp.bfloat16).astype(jnp.float32)
    return first, second, value - first - second


def features(high, low, left, extra):
    full = high.astype(jnp.float32) + low.astype(jnp.float32)
    norm = extra - 0.5 * jnp.sum(full * full, axis=0, keepdims=True)
    first, second, third = three_terms(norm)
    row = lax.broadcasted_iota(jnp.int32, high.shape, 0)
    base = 0 if left else 3
    tail = jnp.where((row >= 3 - base) & (row < 6 - base), 1.0, 0.0)
    tail = jnp.where(row == base, first, tail)
    tail = jnp.where(row == base + 1, second, tail)
    tail = jnp.where(row == base + 2, third, tail)
    tail = tail.astype(jnp.bfloat16)
    pieces = [high, low, high, low, tail] if left else [high, high, low, low, tail]
    return jnp.concatenate(pieces, axis=0)


FEATURES = 5 * DIM
TILE = 512
DEPTH = 2


def exponents(left, right_ref, tile):
    return lax.dot_general(
        left,
        right_ref[:, tile * TILE : (tile + 1) * TILE],
        (((0,), (0,)), ((), ())),
        preferred_element_type=jnp.float32,
    )


def add_rows(sources, right_ref, out_ref):
    work = []
    for source in sources:
        for pair in range(NEAR // 2):
            values, left = [], []
            for j in range(2):
                block = source[pair * 2 + j]
                values.append(block[:COLS])
                left.append(features(block[COLS : COLS + DIM], block[COLS + DIM :], True, 0.0))
            values = jnp.concatenate(values, axis=1)
            left = jnp.concatenate(left, axis=1)
            work += [(values, left, tile) for tile in range(BLK * PART // TILE)]
    ahead = [exponents(left, right_ref, tile) for _, left, tile in work[:DEPTH]]
    for at, (values, _, tile) in enumerate(work):
        if at + DEPTH < len(work):
            ahead.append(exponents(work[at + DEPTH][1], right_ref, work[at + DEPTH][2]))
        entries = jnp.exp2(ahead[at]).astype(jnp.bfloat16)
        part = jnp.dot(values, entries, preferred_element_type=jnp.float32)
        for k in range(TILE // PART):
            out_ref[tile * (TILE // PART) + k] += part[:, k * PART : (k + 1) * PART]


def first_kernel(flat_ref, mine_ref, cols_ref, out_ref, right_ref):
    _, zh, _, zl, x = place(flat_ref[0])
    for peer in range(BLK):
        s, first = peer // 4, 2 * (peer % 4)
        block = jnp.concatenate(
            [cols_ref[first + j, :, s * LANES : (s + 1) * LANES] for j in range(2)], axis=1
        )
        right_ref[:, peer * PART : (peer + 1) * PART] = features(block[:DIM], block[DIM:], False, LOG2AMP)
    out_ref[...] = jnp.zeros_like(out_ref)
    add_rows([mine_ref], right_ref, out_ref)
    inc = noise_var * mine_ref[zh, :COLS, :].astype(jnp.float32)
    for half in range(2):

        @pl.when((x & 1) == half)
        def _():
            for s in range(2):
                at = s * 4 + zl * 2 + lax.shift_right_logical(x, 1)
                out_ref[at, :, half * LANES : (half + 1) * LANES] += inc[:, s * LANES : (s + 1) * LANES]


def second_kernel(right_ref, so_far_ref, a_ref, b_ref, c_ref, out_ref):
    out_ref[...] = so_far_ref[...]
    add_rows([a_ref, b_ref, c_ref], right_ref, out_ref)


def third_kernel(flat_ref, right_ref, so_far_ref, a_ref, b_ref, c_ref, d_ref, out_ref, own_ref, sum_ref):
    _, _, _, zl, x = place(flat_ref[0])
    sum_ref[...] = so_far_ref[...]
    add_rows([a_ref, b_ref, c_ref, d_ref], right_ref, sum_ref)
    out_ref[...] = sum_ref[...].astype(jnp.bfloat16)
    own_ref[...] = sum_ref[zl * 4 + x]


def end_kernel(flat_ref, own_ref, parts_ref, res_ref, out_ref):
    _, _, _, zl, x = place(flat_ref[0])
    change = own_ref[...]
    for peer in range(BLK):
        change += jnp.where(peer == zl * 4 + x, 0.0, parts_ref[peer].astype(jnp.float32))
    for k in range(2):
        old = res_ref[pl.ds(4 * x + 2 * k + zl, COLS, stride=16), :]
        out_ref[:, k * LANES : (k + 1) * LANES] = old - change[:, k * LANES : (k + 1) * LANES]


def exchange(pieces, axes):
    return lax.all_to_all(pieces, axes, split_axis=0, concat_axis=0, tiled=True)


def swap_core(value):
    return lax.ppermute(value, "core", [(0, 1), (1, 0)])


def call(kernel, shapes, scalars, arrays, scratch=(), fetched=(), distant=()):
    return pl.pallas_call(
        kernel,
        out_shape=shapes,
        in_specs=[SM] * len(scalars) + [ANY] * len(distant) + [VM] * (len(fetched) + len(arrays)),
        out_specs=jax.tree.map(lambda _: VM, shapes),
        scratch_shapes=scratch,
        compiler_params=pltpu.CompilerParams(vmem_limit_bytes=KERNEL_VMEM),
    )(
        *[pltpu.with_memory_space_constraint(a, pltpu.HBM) for a in [*scalars, *distant, *fetched]],
        *[pltpu.with_memory_space_constraint(a, pltpu.VMEM) for a in arrays],
    )


def per_device(points, lengthscales, point_order, block_slot, block_inverses, residual):
    f32, bf16, shape, whole = jnp.float32, jnp.bfloat16, pltpu.VMEM, jax.ShapeDtypeStruct
    flat = lax.axis_index(AXES).astype(jnp.int32)[None]
    rows = residual.reshape(COLS, 2, BS // LANES, LANES).transpose(0, 2, 1, 3).reshape(-1, LANES)
    start = call(
        start_kernel,
        shape((PLANE, 2 * DIM, PART), bf16),
        [lengthscales],
        [],
        fetched=[points],
    )
    mine = exchange(start, ("y", "x"))
    other = swap_core(mine)
    increments, flat_inc = call(
        solve_kernel,
        (whole((COLS, 2, LANES), bf16), shape((COLS, PART), bf16)),
        [],
        [rows],
        [pltpu.VMEM((2, LANES, BS), bf16), pltpu.SemaphoreType.DMA((8,))],
        distant=[block_inverses],
    )
    picked = call(
        pick_kernel,
        shape((BLK, 2 * DIM, PART), bf16),
        [flat, block_slot],
        [point_order.reshape(-1, LANES), mine, other, flat_inc],
    )
    packed, cols = call(
        pack_kernel,
        (shape((NEAR, COLS + 2 * DIM, PART), bf16), shape((BLK, 2 * DIM, PART), bf16)),
        [],
        [exchange(picked, ("zh", "zl")), flat_inc],
    )
    taken = exchange(packed, "zh")
    moved = [lax.ppermute(taken, "y", [(k, (k + shift) % 4) for k in range(4)]) for shift in (1, 3, 2)]
    cols = exchange(cols, ("zl", "x"))
    swapped = [swap_core(value) for value in [taken, *moved]]
    partial, right = call(
        first_kernel,
        (shape((BLK, COLS, PART), f32), shape((FEATURES, BLK * PART), bf16)),
        [flat],
        [taken, cols],
    )
    partial = call(second_kernel, shape((BLK, COLS, PART), f32), [], [right, partial, *moved])
    partial, own = call(
        third_kernel,
        (shape((BLK, COLS, PART), bf16), shape((COLS, PART), f32)),
        [flat],
        [right, partial, *swapped],
        [pltpu.VMEM((BLK, COLS, PART), f32)],
    )
    parts = exchange(partial, ("zl", "x"))
    return increments, call(end_kernel, whole((COLS, PART), f32), [flat], [own, parts, rows])


def solution(mesh):
    fine = Mesh(np.asarray(mesh.devices).reshape(SIZES), AXES)
    row, blk = ("y", "zh", "core"), ("zl", "x")
    return jax.shard_map(
        per_device,
        mesh=fine,
        in_specs=(P(None, AXES), P(), P(), P(), P(row, blk, None), P(None, row, None)),
        out_specs=(P(None, row, blk), P(None, AXES)),
        check_vma=False,
    )
```

```python
import math

import jax
import jax.numpy as jnp
import numpy as np
from jax import lax
from jax.experimental import pallas as pl
from jax.experimental.pallas import tpu as pltpu
from jax.sharding import Mesh
from jax.sharding import PartitionSpec as P

damping = 0.5
amplitude = 0.3
noise_var = 0.25

AXES = ("y", "zh", "core", "zl", "x")
SIZES = (4, 4, 2, 2, 4)
DIM = 16
COLS = 64
PART = 256
BS = 1024
NBLK = 64
LANES = 128
BLK = 8
NEAR = 4
PLANE = 16
KERNEL_VMEM = 16 << 20
LOG2E = math.log2(math.e)
LOG2AMP = math.log2(amplitude)

VM = pl.BlockSpec(memory_space=pltpu.VMEM)
SM = pl.BlockSpec(memory_space=pltpu.SMEM)


def place(f):
    return (
        lax.shift_right_logical(f, 6),
        lax.shift_right_logical(f, 4) & 3,
        lax.shift_right_logical(f, 3) & 1,
        lax.shift_right_logical(f, 2) & 1,
        f & 3,
    )


def solve_kernel(inv_ref, res_ref, flat_ref):
    for s in range(2):
        low = [res_ref[pl.ds(2 * j + s, COLS, stride=16), :].astype(jnp.bfloat16) for j in range(BS // LANES)]
        solved = lax.dot_general(
            jnp.concatenate(low, axis=1),
            inv_ref[s],
            (((1,), (1,)), ((), ())),
            preferred_element_type=jnp.float32,
        )
        flat_ref[:, s * LANES : (s + 1) * LANES] = (damping * solved).astype(jnp.bfloat16)


def keep_kernel(flat_ref, _, inc_ref):
    for s in range(2):
        inc_ref[:, s, :] = flat_ref[:, s * LANES : (s + 1) * LANES]


def start_kernel(scale_ref, points_ref, out_ref):
    scale = jnp.concatenate([jnp.full((1, PART), scale_ref[d], jnp.float32) for d in range(DIM)], axis=0)
    own = (points_ref[...] - 0.5) * (math.sqrt(LOG2E) / scale)
    high = own.astype(jnp.bfloat16)
    low = (own - high.astype(jnp.float32)).astype(jnp.bfloat16)
    for dev in range(PLANE):
        out_ref[dev, :DIM, :] = high
        out_ref[dev, DIM:, :] = low


def pick_kernel(flat_ref, slot_ref, order_ref, mine_ref, other_ref, _, out_ref):
    y, zh, core, zl, x = place(flat_ref[0])
    member = lax.broadcasted_iota(jnp.int32, (PART, 2 * PART), 0)

    def two_peers(pair, carry):
        slot = 2 * ((y * 4 + pair) * 2 + core)
        wanted = [slot_ref[slot + s] * 8 + peer_zl * 4 + x for peer_zl in range(2) for s in range(2)]
        p = jnp.concatenate([order_ref[pl.ds(row, 1), :] for row in wanted], axis=1)
        gy, gzh, gcore, gzl, gx = place(lax.shift_right_logical(p, 8))
        here = (gzh == zh) & (gzl == zl)
        holder = jnp.where(here, ((gcore ^ core) * 4 + gy) * 4 + gx, -1)
        chosen = (member == (p & (PART - 1))).astype(jnp.bfloat16)
        holder = jnp.broadcast_to(holder, (2 * DIM, 2 * PART))
        found = jnp.zeros((2 * DIM, 2 * PART), jnp.float32)
        for source in range(2):
            table = (other_ref if source else mine_ref)[...].reshape(PLANE * 2 * DIM, PART)
            taken = jnp.dot(table, chosen, preferred_element_type=jnp.float32)
            for dev in range(PLANE):
                rows = taken[dev * 2 * DIM : (dev + 1) * 2 * DIM]
                found = jnp.where(holder == source * PLANE + dev, rows, found)
        found = found.astype(jnp.bfloat16)
        out_ref[2 * pair] = found[:, :PART]
        out_ref[2 * pair + 1] = found[:, PART:]
        return carry

    lax.fori_loop(0, BLK // 2, two_peers, 0, unroll=4)


def pack_kernel(parts_ref, inc_ref, rows_ref, cols_ref):
    total = parts_ref[0].astype(jnp.float32)
    for peer in range(1, BLK):
        total += parts_ref[peer].astype(jnp.float32)
    total = total.astype(jnp.bfloat16)
    inc = inc_ref[...]
    for dev in range(NEAR):
        rows_ref[dev, :COLS, :] = inc
        rows_ref[dev, COLS:, :] = total
    for dev in range(BLK):
        cols_ref[dev] = total


def three_terms(value):
    first = value.astype(jnp.bfloat16).astype(jnp.float32)
    second = (value - first).astype(jnp.bfloat16).astype(jnp.float32)
    return first, second, value - first - second


def features(high, low, left, extra):
    full = high.astype(jnp.float32) + low.astype(jnp.float32)
    norm = extra - 0.5 * jnp.sum(full * full, axis=0, keepdims=True)
    first, second, third = three_terms(norm)
    row = lax.broadcasted_iota(jnp.int32, high.shape, 0)
    base = 0 if left else 3
    tail = jnp.where((row >= 3 - base) & (row < 6 - base), 1.0, 0.0)
    tail = jnp.where(row == base, first, tail)
    tail = jnp.where(row == base + 1, second, tail)
    tail = jnp.where(row == base + 2, third, tail)
    tail = tail.astype(jnp.bfloat16)
    pieces = [high, low, high, low, tail] if left else [high, high, low, low, tail]
    return jnp.concatenate(pieces, axis=0)


FEATURES = 5 * DIM
TILE = 512
DEPTH = 1


def exponents(left, right_ref, tile):
    return lax.dot_general(
        left,
        right_ref[:, tile * TILE : (tile + 1) * TILE],
        (((0,), (0,)), ((), ())),
        preferred_element_type=jnp.float32,
    )


def add_rows(sources, right_ref, out_ref):
    work = []
    for source in sources:
        for pair in range(NEAR // 2):
            values, left = [], []
            for j in range(2):
                block = source[pair * 2 + j]
                values.append(block[:COLS])
                left.append(features(block[COLS : COLS + DIM], block[COLS + DIM :], True, 0.0))
            values = jnp.concatenate(values, axis=1)
            left = jnp.concatenate(left, axis=1)
            work += [(values, left, tile) for tile in range(BLK * PART // TILE)]
    ahead = [exponents(left, right_ref, tile) for _, left, tile in work[:DEPTH]]
    for at, (values, _, tile) in enumerate(work):
        if at + DEPTH < len(work):
            ahead.append(exponents(work[at + DEPTH][1], right_ref, work[at + DEPTH][2]))
        entries = jnp.exp2(ahead[at]).astype(jnp.bfloat16)
        part = jnp.dot(values, entries, preferred_element_type=jnp.float32)
        for k in range(TILE // PART):
            out_ref[tile * (TILE // PART) + k] += part[:, k * PART : (k + 1) * PART]


def first_kernel(flat_ref, mine_ref, cols_ref, out_ref, right_ref):
    _, zh, _, zl, x = place(flat_ref[0])
    for peer in range(BLK):
        s, first = peer // 4, 2 * (peer % 4)
        block = jnp.concatenate(
            [cols_ref[first + j, :, s * LANES : (s + 1) * LANES] for j in range(2)], axis=1
        )
        right_ref[:, peer * PART : (peer + 1) * PART] = features(block[:DIM], block[DIM:], False, LOG2AMP)
    out_ref[...] = jnp.zeros_like(out_ref)
    add_rows([mine_ref], right_ref, out_ref)
    inc = noise_var * mine_ref[zh, :COLS, :].astype(jnp.float32)
    for half in range(2):

        @pl.when((x & 1) == half)
        def _():
            for s in range(2):
                at = s * 4 + zl * 2 + lax.shift_right_logical(x, 1)
                out_ref[at, :, half * LANES : (half + 1) * LANES] += inc[:, s * LANES : (s + 1) * LANES]


def second_kernel(right_ref, so_far_ref, a_ref, b_ref, c_ref, out_ref):
    out_ref[...] = so_far_ref[...]
    add_rows([a_ref, b_ref, c_ref], right_ref, out_ref)


def third_kernel(flat_ref, right_ref, so_far_ref, a_ref, b_ref, c_ref, d_ref, out_ref, own_ref, sum_ref):
    _, _, _, zl, x = place(flat_ref[0])
    sum_ref[...] = so_far_ref[...]
    add_rows([a_ref, b_ref, c_ref, d_ref], right_ref, sum_ref)
    out_ref[...] = sum_ref[...].astype(jnp.bfloat16)
    own_ref[...] = sum_ref[zl * 4 + x]


def end_kernel(flat_ref, own_ref, parts_ref, res_ref, out_ref):
    _, _, _, zl, x = place(flat_ref[0])
    change = own_ref[...]
    for peer in range(BLK):
        change += jnp.where(peer == zl * 4 + x, 0.0, parts_ref[peer].astype(jnp.float32))
    for k in range(2):
        old = res_ref[pl.ds(4 * x + 2 * k + zl, COLS, stride=16), :]
        out_ref[:, k * LANES : (k + 1) * LANES] = old - change[:, k * LANES : (k + 1) * LANES]


def exchange(pieces, axes):
    return lax.all_to_all(pieces, axes, split_axis=0, concat_axis=0, tiled=True)


def swap_core(value):
    return lax.ppermute(value, "core", [(0, 1), (1, 0)])


def call(kernel, shapes, scalars, arrays, scratch=(), fetched=()):
    return pl.pallas_call(
        kernel,
        out_shape=shapes,
        in_specs=[SM] * len(scalars) + [VM] * (len(fetched) + len(arrays)),
        out_specs=jax.tree.map(lambda _: VM, shapes),
        scratch_shapes=scratch,
        compiler_params=pltpu.CompilerParams(vmem_limit_bytes=KERNEL_VMEM),
    )(
        *[pltpu.with_memory_space_constraint(a, pltpu.HBM) for a in [*scalars, *fetched]],
        *[pltpu.with_memory_space_constraint(a, pltpu.VMEM) for a in arrays],
    )


def per_device(points, lengthscales, point_order, block_slot, block_inverses, residual):
    f32, bf16, shape, whole = jnp.float32, jnp.bfloat16, pltpu.VMEM, jax.ShapeDtypeStruct
    flat = lax.axis_index(AXES).astype(jnp.int32)[None]
    rows = residual.reshape(COLS, 2, BS // LANES, LANES).transpose(0, 2, 1, 3).reshape(-1, LANES)
    start = call(
        start_kernel,
        shape((PLANE, 2 * DIM, PART), bf16),
        [lengthscales],
        [],
        fetched=[points],
    )
    mine = exchange(start, ("y", "x"))
    other = swap_core(mine)
    flat_inc = call(solve_kernel, shape((COLS, PART), bf16), [], [rows], fetched=[block_inverses])
    picked = call(
        pick_kernel,
        shape((BLK, 2 * DIM, PART), bf16),
        [flat, block_slot],
        [point_order.reshape(-1, LANES), mine, other, flat_inc],
    )
    packed, cols = call(
        pack_kernel,
        (shape((NEAR, COLS + 2 * DIM, PART), bf16), shape((BLK, 2 * DIM, PART), bf16)),
        [],
        [exchange(picked, ("zh", "zl")), flat_inc],
    )
    taken = exchange(packed, "zh")
    moved = [lax.ppermute(taken, "y", [(k, (k + shift) % 4) for k in range(4)]) for shift in (1, 3, 2)]
    cols = exchange(cols, ("zl", "x"))
    swapped = [swap_core(value) for value in [taken, *moved]]
    increments = call(keep_kernel, whole((COLS, 2, LANES), bf16), [], [flat_inc, taken])
    increments, cols = lax.optimization_barrier((increments, cols))
    partial, right = call(
        first_kernel,
        (shape((BLK, COLS, PART), f32), shape((FEATURES, BLK * PART), bf16)),
        [flat],
        [taken, cols],
    )
    partial = call(second_kernel, shape((BLK, COLS, PART), f32), [], [right, partial, *moved])
    partial, own = call(
        third_kernel,
        (shape((BLK, COLS, PART), bf16), shape((COLS, PART), f32)),
        [flat],
        [right, partial, *swapped],
        [pltpu.VMEM((BLK, COLS, PART), f32)],
    )
    parts = exchange(partial, ("zl", "x"))
    return increments, call(end_kernel, whole((COLS, PART), f32), [flat], [own, parts, rows])


def solution(mesh):
    fine = Mesh(np.asarray(mesh.devices).reshape(SIZES), AXES)
    row, blk = ("y", "zh", "core"), ("zl", "x")
    return jax.shard_map(
        per_device,
        mesh=fine,
        in_specs=(P(None, AXES), P(), P(), P(), P(row, blk, None), P(None, row, None)),
        out_specs=(P(None, row, blk), P(None, AXES)),
        check_vma=False,
    )
```
